32 devices in a mesh: clip: 2 (over y), tile: 4 (over z), tm: 2 (over x), chan: 2 (over core).
Axes of the slice: x: 2, y: 2, z: 4, core: 2. Of those that a mesh axis runs over, the one named last changes fastest.
Arguments:
- latent: bfloat16 [8, 8, 256, 128], P(('clip', 'tm'), 'tile', 'chan'), parts along dimension 0
- norm1_gain: float32 [256], P('chan'), may hold values from 0.25 to 1.75
- norm1_bias: float32 [256], P('chan'), may hold values from -3 to 3
- conv1_weight: bfloat16 [3, 3, 3, 256, 256], P(None, None, None, None, 'chan'), may hold values from -0.078125 to 0.078125
- conv1_bias: float32 [256], P('chan'), may hold values from -3 to 3
- norm2_gain: float32 [256], P('chan'), may hold values from 0.25 to 1.75
- norm2_bias: float32 [256], P('chan'), may hold values from -3 to 3
- conv2_weight: bfloat16 [3, 3, 3, 256, 256], P(None, None, None, None, 'chan'), may hold values from -0.078125 to 0.078125
- conv2_bias: float32 [256], P('chan'), may hold values from -3 to 3
Outputs:
- upsampled: bfloat16 [8, 16, 64, 256], P(('clip', 'tm'), 'tile', 'chan'), parts along dimension 0
The draws below stay inside these ranges and needn't reach their ends.
There are 2 independent parts, one for each index of `clip`. The reference program is written for one: setup_inputs(seed, part) draws one part's arguments, and reference() takes and returns one part's arrays. A program takes and returns all parts, laid end to end along the dimension named above; an argument that names none is the same for every part. Nothing has to cross between parts.
All inputs are finite; a program needn't handle non-finite values.
Results may differ from the reference program's by a relative error of at most 0.0026.
Values may be sent and summed in bfloat16 or wider, within the bound.
A program may use at most 64 MiB of HBM per device.

```python
import jax
import jax.numpy as jnp
from jax import lax

C = 256
GROUPS = 32
WIDE = 128
FRAMES = 4
HEIGHT = 8


def draw_latent(key, part):
    keys = jax.random.split(key, 3)
    shape = (FRAMES, HEIGHT, C, WIDE)
    rows = jnp.arange(HEIGHT, dtype=jnp.float32) / float(max(HEIGHT - 1, 1))
    rough = jax.random.uniform(keys[1], (HEIGHT,), jnp.float32, 0.6, 1.4)
    offset = jax.random.uniform(keys[2], (FRAMES, 1, C, 1), jnp.float32, -0.6, 0.6)
    base = jax.random.normal(keys[0], shape, jnp.float32)
    row_scale = jnp.exp(jnp.log(3.0) * rows) * rough
    values = base * row_scale[None, :, None, None] + offset
    return values.astype(jnp.bfloat16)


def block_scale(stream_key, dims, pieces, least, top_value):
    loudness = 1.0
    for axis_at, shards_of in pieces:
        steps = jax.random.uniform(jax.random.fold_in(jax.random.fold_in(stream_key, 6), axis_at), (shards_of,), jnp.float32, least / len(pieces), top_value / len(pieces))
        loudness = loudness * jnp.repeat(jnp.exp(steps), dims[axis_at] // shards_of).reshape((-1,) + (1,) * (len(dims) - 1 - axis_at))
    return loudness


def scatter_about(rng, extent, spread, most, cuts=(), held_as=jnp.bfloat16):
    values = spread * jax.random.normal(rng, extent, jnp.float32)
    if cuts:
        values = values * block_scale(rng, extent, cuts, -0.22, 0.18)
    return jnp.clip(values, -most, most).astype(held_as)


def setup_inputs(seed: int = 0, part: int = 0) -> dict:
    seeds = jax.random.split(jax.random.key(seed), 10)
    part_keys = jax.random.split(jax.random.fold_in(seeds[9], part), 10)
    return {
        "latent": draw_latent(jax.random.fold_in(jax.random.fold_in(seeds[9], part), 71), part),
        "norm1_gain": jnp.clip(1.0 + 0.15 * jax.random.normal(seeds[1], (C,), jnp.float32), 0.25, 1.75),
        "norm1_bias": scatter_about(seeds[2], (C,), 0.5, 3.0, ((0, 2),), jnp.float32),
        "conv1_weight": scatter_about(seeds[3], (3, 3, 3, C, C), (27 * C) ** -0.5, 0.078125, ((4, 2),)),
        "conv1_bias": scatter_about(seeds[4], (C,), 0.5, 3.0, ((0, 2),), jnp.float32),
        "norm2_gain": jnp.clip(1.0 + 0.15 * jax.random.normal(seeds[5], (C,), jnp.float32), 0.25, 1.75),
        "norm2_bias": scatter_about(seeds[6], (C,), 0.5, 3.0, ((0, 2),), jnp.float32),
        "conv2_weight": scatter_about(seeds[7], (3, 3, 3, C, C), (27 * C) ** -0.5, 0.078125, ((4, 2),)),
        "conv2_bias": scatter_about(seeds[8], (C,), 0.5, 3.0, ((0, 2),), jnp.float32),
    }


def causal_norm(field, gain, bias):
    frames, height, channels, columns = field.shape
    size = channels // GROUPS
    parts = field.reshape(frames, height, GROUPS, size, columns)
    totals = jnp.cumsum(lax.optimization_barrier(jnp.sum(parts, axis=(1, 3, 4))), axis=0)
    squares = jnp.cumsum(lax.optimization_barrier(jnp.sum(parts * parts, axis=(1, 3, 4))), axis=0)
    count = (jnp.arange(frames, dtype=jnp.float32) + 1.0) * float(height * size * columns)
    mean = totals / count[:, None]
    var = squares / count[:, None] - mean * mean
    scale = 1.0 / jnp.sqrt(var + 1e-06)
    normed = (parts - mean[:, None, :, None, None]) * scale[:, None, :, None, None]
    normed = normed.reshape(frames, height, channels, columns)
    return normed * gain[None, None, :, None] + bias[None, None, :, None]

def causal_conv(field, weight, bias):
    padded = jnp.concatenate([field[0:1], field[0:1], field], axis=0)
    source = jnp.transpose(padded, (2, 0, 1, 3))[None]
    result = lax.conv_general_dilated(source, weight, (1, 1, 1), ((0, 0), (1, 1), (1, 1)), dimension_numbers=('NCDHW', 'DHWIO', 'NCDHW'), preferred_element_type=jnp.float32)
    result = jnp.transpose(result[0], (1, 2, 0, 3))
    return result + bias[None, None, :, None]

def reference(latent, norm1_gain, norm1_bias, conv1_weight, conv1_bias, norm2_gain, norm2_bias, conv2_weight, conv2_bias):
    source = latent.astype(jnp.float32)
    first = jax.nn.silu(causal_norm(source, norm1_gain, norm1_bias)).astype(jnp.bfloat16)
    hidden = causal_conv(first, conv1_weight, conv1_bias)
    second = jax.nn.silu(causal_norm(hidden, norm2_gain, norm2_bias)).astype(jnp.bfloat16)
    mixed = source + causal_conv(second, conv2_weight, conv2_bias)
    frames, height, channels, columns = mixed.shape
    shaped = mixed.reshape(frames, height, channels // 4, 2, 2, columns)
    shaped = jnp.transpose(shaped, (0, 1, 3, 2, 5, 4))
    return shaped.reshape(frames, 2 * height, channels // 4, 2 * columns).astype(jnp.bfloat16)
```

```python
import functools

import jax
import jax.numpy as jnp
from jax import lax
from jax.experimental import pallas as pl
from jax.experimental.pallas import tpu as pltpu
from jax.sharding import PartitionSpec as P

MESH = pl.DeviceIdType.MESH
C = 256
GROUPS = 32
SIZE = C // GROUPS
F32 = jnp.float32
BF16 = jnp.bfloat16


def iota(shape, dim):
    return lax.broadcasted_iota(jnp.int32, shape, dim)


def column(row, n):
    wide = jnp.broadcast_to(row, (n, row.shape[-1]))
    return jnp.sum(jnp.where(iota(wide.shape, 0) == iota(wide.shape, 1), wide, 0.0), axis=1, keepdims=True)


def kernel(
    tiles,
    blocks,
    latent,
    n1g,
    n1b,
    w1,
    c1b,
    n2g,
    n2b,
    w2,
    c2b,
    out,
    w1v,
    w2v,
    w1t,
    w2t,
    lat,
    act1,
    hid,
    hsend,
    hedge,
    act2,
    mix,
    select,
    params,
    cols,
    affine,
    own_stats,
    stats,
    l_sem,
    w_sem,
    x_send,
    z_send,
    a_recv,
    d_send,
    d_recv,
    hz_send,
    h_recv,
    e_send,
    e_recv,
    s_send,
    s_recv,
):
    tm = lax.axis_index("tm")
    tile = lax.axis_index("tile")
    core = lax.axis_index("chan")
    other = 1 - core
    me = tm * tiles + tile
    local = latent.shape[2]
    wide = latent.shape[3]
    groups = local // SIZE
    rows = latent.shape[1]

    def remote(src, dst, send, recv, **device):
        return pltpu.make_async_remote_copy(
            src_ref=src, dst_ref=dst, send_sem=send, recv_sem=recv, device_id=device, device_id_type=MESH
        )

    def when(condition, action):
        @pl.when(condition)
        def _():
            action()

    def each_peer(b, action):
        def one(t, carry):
            when(jnp.logical_or(t != tile, b != tm), lambda: action(t))
            return carry

        lax.fori_loop(0, tiles, one, 0)

    barrier = pltpu.get_barrier_semaphore()
    pl.semaphore_signal(barrier, inc=1, device_id={"chan": other}, device_id_type=MESH)
    for b in range(blocks):
        each_peer(b, lambda t, b=b: pl.semaphore_signal(
            barrier, inc=1, device_id={"tm": b, "tile": t}, device_id_type=MESH))

    loads = [pltpu.make_async_copy(latent, lat.at[2, :, 1:3], l_sem.at[0])]
    loads += [
        pltpu.make_async_copy(ref, params.at[i], l_sem.at[1 + i])
        for i, ref in enumerate((n1g, n1b, n2g, n2b, c1b, c2b))
    ]
    load1 = pltpu.make_async_copy(w1, w1v, w_sem.at[0])
    load2 = pltpu.make_async_copy(w2, w2v, w_sem.at[1])
    for copy in loads:
        copy.start()
    load1.start()
    load2.start()

    started = []

    def go(condition, copy):
        @pl.when(condition)
        def _():
            copy.start()

        started.append((condition, copy))

    always = core >= 0
    has_up = tile < tiles - 1
    has_down = tile > 0
    slots = [s for s in range(3) if blocks > 2 - s]
    before = [s for s in slots if s < 2]

    def row_here(row):
        return has_down if row == 0 else has_up if row == 3 else always

    def lat_copy(src, s, row, f, send, **device):
        return remote(src, lat.at[s, f, row], send, a_recv.at[s, row, f], **device)

    lanes = iota((groups, 128), 1)
    subs = iota((groups, 128), 0)

    def make_stats(which, field):
        row = jnp.zeros((1, 128), F32)
        for f in (0, 1):
            total = jnp.zeros((groups, wide), F32)
            square = jnp.zeros((groups, wide), F32)
            for r in (0, 1):
                v = field(f, r).reshape(groups, SIZE, wide)
                total = total + jnp.sum(v, axis=1)
                square = square + jnp.sum(v * v, axis=1)
            for kind, part in enumerate((total, square)):
                col = jnp.sum(part, axis=1, keepdims=True)
                at = kind * 2 * groups + f * groups
                row = row + jnp.sum(jnp.where(lanes == subs + at, col, 0.0), axis=0, keepdims=True)
        own_stats[which] = row
        stats[which, me] = row

    def stats_to(which, b, t):
        return remote(own_stats.at[which], stats.at[which, me], s_send.at[which, b * tiles + t],
                      s_recv.at[which, me], tm=b, tile=t)

    def send_stats(which):
        for b in range(blocks):
            when(b >= tm, lambda b=b: each_peer(b, lambda t: stats_to(which, b, t).start()))

    def wait_stats(which):
        for b in range(blocks):
            when(b <= tm, lambda b=b: each_peer(b, lambda t: remote(
                own_stats.at[which], stats.at[which, b * tiles + t], s_send.at[which, b * tiles + t],
                s_recv.at[which, b * tiles + t], tm=b, tile=t).wait_recv()))

    def make_norms(which, first_frame, frames, gain, bias, shift):
        ahead = frames // 2 - 1
        per_block = []
        for b in range(blocks):
            first = jnp.sum(stats[which, pl.ds(b * tiles, tiles)], axis=0)
            both = first + pltpu.roll(first, 128 - groups, 1)
            per_block.append((b, first, both))
        for e in range(first_frame, frames):
            block = tm - ahead + e // 2
            later = jnp.logical_and(block >= 0, e % 2 == 1)
            block = jnp.maximum(block, 0)
            number = (block * 2 + later.astype(jnp.int32) + 1).astype(F32)
            count = number * float(rows * tiles * SIZE * wide)
            run = jnp.zeros((1, 128), F32)
            for b, first, both in per_block:
                whole = jnp.logical_or(b < block, jnp.logical_and(b == block, later))
                run = run + jnp.where(whole, both, jnp.where(b == block, first, 0.0))
            mean = run / count
            var = pltpu.roll(mean, 128 - 2 * groups, 1) - mean * mean
            scale = 1.0 / jnp.sqrt(var + 1e-06)
            diagonal = lanes == subs

            def spread_out(value):
                col = jnp.sum(jnp.where(diagonal, jnp.broadcast_to(value, lanes.shape), 0.0), axis=1, keepdims=True)
                return jnp.broadcast_to(col[:, :, None], (groups, SIZE, 128)).reshape(local, 128)

            slope = spread_out(scale) * cols[gain]
            offset = -spread_out(mean)
            if shift is not None:
                offset = offset + cols[shift]
            affine[e, 0] = slope
            affine[e, 1] = cols[bias] + offset * slope

    def flip(src, dst):
        def one(j, carry):
            for i in range(3):
                for k in range(3):
                    dst[j, k * local:(k + 1) * local, i * C:(i + 1) * C] = src[i, j, k].T
            return carry

        lax.fori_loop(0, 3, one, 0)

    def silu_of_twice(half):
        return half + half * jnp.tanh(half)

    def part_of(act, row, e, which):
        return act.at[row, pl.ds(pl.multiple_of(e * C + which * local, local), local)]

    def normed(act, send, recv, e, row, value):
        v = silu_of_twice(value * affine[e, 0] + affine[e, 1])
        mine = part_of(act, row, e, core)
        mine[...] = v.astype(BF16)
        remote(mine, mine, send.at[row, e], recv.at[row, e], chan=other).start()

    def of_other(act, send, recv, e, row):
        return remote(part_of(act, row, e, core), part_of(act, row, e, other), send.at[row, e], recv.at[row, e],
                      chan=other)

    def repeat(act, e, to):
        for row in range(4):
            v = act[row, e * C:(e + 1) * C]
            for at in to:
                act[row, at * C:(at + 1) * C] = v

    def clear_edges(act):
        for side, row in ((has_down, 0), (has_up, 3)):
            @pl.when(jnp.logical_not(side))
            def _(row=row):
                act[row] = jnp.zeros(act.shape[1:], BF16)

    def conv(act, wt, o):
        acc = None
        at = pl.ds(pl.multiple_of(o * C, C), 3 * C)
        taps = [act[row, at] for row in range(4)]
        for j in range(3):
            part = jnp.dot(wt[j], jnp.concatenate(taps[j:j + 2], axis=1), preferred_element_type=F32)
            acc = part if acc is None else acc + part
        lane = iota((local, wide), 1)
        result = []
        for r in range(2):
            a = [acc[k * local:(k + 1) * local, r * wide:(r + 1) * wide] for k in range(3)]
            left = jnp.where(lane == 0, 0.0, pltpu.roll(a[0], 1, 1))
            right = jnp.where(lane == wide - 1, 0.0, pltpu.roll(a[2], wide - 1, 1))
            result.append(a[1] + left + right)
        return result

    pl.semaphore_wait(barrier, blocks * tiles)

    for s in reversed(before):
        for f in (0, 1):
            for r in (0, 1):
                go(tm + (2 - s) < blocks,
                   lat_copy(latent.at[f, r], s, 1 + r, f, x_send.at[s, r, f], tm=tm + (2 - s)))
    for f in (0, 1):
        go(has_up, lat_copy(latent.at[f, 1], 2, 0, f, z_send.at[2, 0, f], tile=tile + 1))
        go(has_down, lat_copy(latent.at[f, 0], 2, 3, f, z_send.at[2, 1, f], tile=tile - 1))

    for copy in loads:
        copy.wait()
    make_stats(0, lambda f, r: lat[2, f, 1 + r].astype(F32))
    send_stats(0)

    clear_edges(act1)
    clear_edges(act2)
    for i, factor in enumerate((0.5, 0.5, 0.5, 0.5, 1.0, 1.0)):
        cols[i] = jnp.broadcast_to(column(factor * params[i], local), (local, 128))
    a, b = iota((2 * wide, 2 * wide), 0), iota((2 * wide, 2 * wide), 1)
    select[...] = jnp.where(b == 2 * (a % wide) + a // wide, 1.0, 0.0).astype(BF16)
    load1.wait()
    flip(w1v, w1t)
    load2.wait()
    flip(w2v, w2t)

    def arrived(s, row, f):
        lat_copy(lat.at[s, f, row], s, row, f, z_send.at[2, 0, 0], tile=tile).wait_recv()

    for s in reversed(before):
        here = tm >= 2 - s
        for f in (0, 1):
            for r in (0, 1):
                when(here, functools.partial(arrived, s, 1 + r, f))
                side, row, to = ((has_down, 3, tile - 1), (has_up, 0, tile + 1))[r]
                go(jnp.logical_and(here, side),
                   lat_copy(lat.at[s, f, 1 + r], s, row, f, z_send.at[s, 1 - r, f], tile=to))

    wait_stats(0)
    make_norms(0, 6 - 2 * len(slots), 6, 0, 1, None)

    def norm1(s, f, row):
        e = 2 * s + f
        normed(act1, d_send, d_recv, e, row, lat[s, f, row].astype(F32))

    def norm1_inner(s):
        def one(step, carry):
            norm1(s, step // 2, 1 + step % 2)
            return carry

        lax.fori_loop(0, 4, one, 0)

    norm1_inner(2)
    for s in before:
        when(tm >= 2 - s, functools.partial(norm1_inner, s))

    for s in reversed(slots):
        for f in (0, 1):
            for row in (0, 3):
                @pl.when(jnp.logical_and(tm >= 2 - s, row_here(row)))
                def _(s=s, f=f, row=row):
                    arrived(s, row, f)
                    norm1(s, f, row)

    def frames1(action):
        for s in reversed(slots):
            for f in (0, 1):
                for row in (1, 2, 0, 3):
                    when(jnp.logical_and(tm >= 2 - s, row_here(row)),
                        lambda e=2 * s + f, row=row: action(of_other(act1, d_send, d_recv, e, row)))

    frames1(lambda copy: copy.wait_recv())

    when(tm == 0, lambda: repeat(act1, 4, (3, 2)))
    when(tm == 1, lambda: repeat(act1, 2, (1, 0)))

    def z_copy(o, up):
        at, r, to = (0, 1, tile + 1) if up else (1, 0, tile - 1)
        return remote(hsend.at[r, o], hedge.at[at, o], hz_send.at[at, o], h_recv.at[at, o], tile=to)

    def conv1(o, carry):
        for r, h in enumerate(conv(act1, w1t, o)):
            hid[o, r] = h
            hsend[r, o] = h.astype(BF16)

        when(has_up, lambda: z_copy(o, True).start())
        when(has_down, lambda: z_copy(o, False).start())
        return carry

    lax.fori_loop(2, 4, conv1, 0)
    make_stats(1, lambda f, r: hid[2 + f, r] + cols[4])
    send_stats(1)
    when(tm > 0, lambda: lax.fori_loop(0, 2, conv1, 0))

    wait_stats(1)
    make_norms(1, 0, 4, 2, 3, 4)

    def norm2_inner(first, steps):
        def one(step, carry):
            o, r = first + step // 2, step % 2
            normed(act2, e_send, e_recv, o, 1 + r, hid[o, r])
            return carry

        lax.fori_loop(0, steps, one, 0)

    def made(o):
        return always if o >= 2 else tm > 0

    norm2_inner(2, 4)
    when(tm > 0, lambda: norm2_inner(0, 4))

    for o in (2, 3, 0, 1):
        for at, row in ((0, 0), (1, 3)):
            @pl.when(jnp.logical_and(made(o), row_here(row)))
            def _(o=o, at=at, row=row):
                remote(hsend.at[at, o], hedge.at[at, o], hz_send.at[at, o], h_recv.at[at, o], tile=tile).wait_recv()
                normed(act2, e_send, e_recv, o, row, hedge[at, o].astype(F32))

    def frames2(action):
        for o in (2, 3, 0, 1):
            for row in (1, 2, 0, 3):
                when(jnp.logical_and(made(o), row_here(row)),
                    lambda o=o, row=row: action(of_other(act2, e_send, e_recv, o, row)))

    frames2(lambda copy: copy.wait_recv())
    when(tm == 0, lambda: repeat(act2, 2, (1, 0)))

    def conv2(o, carry):
        for r, h in enumerate(conv(act2, w2t, o)):
            mix[o * 2 + r] = lat[2, o, 1 + r].astype(F32) + (h + cols[5])
        return carry

    lax.fori_loop(0, 2, conv2, 0)

    spread = select[...]
    for f in range(2):
        for r in range(2):
            for p in range(2):
                pair = [mix[f * 2 + r, pl.ds(2 * p + q, local // 4, stride=4), :].astype(BF16) for q in range(2)]
                out[f, 2 * r + p] = jnp.dot(
                    jnp.concatenate(pair, axis=1), spread, preferred_element_type=F32
                ).astype(BF16)

    for condition, copy in started:
        @pl.when(condition)
        def _(copy=copy):
            copy.wait_send()

    for o in range(4):
        for up, side in ((True, has_up), (False, has_down)):
            when(jnp.logical_and(made(o), side), lambda o=o, up=up: z_copy(o, up).wait_send())
    frames1(lambda copy: copy.wait_send())
    frames2(lambda copy: copy.wait_send())
    for which in (0, 1):
        for b in range(blocks):
            when(b >= tm, lambda b=b, which=which: each_peer(b, lambda t: stats_to(which, b, t).wait_send()))


def shards(tiles, blocks, latent, n1g, n1b, w1, c1b, n2g, n2b, w2, c2b):
    frames, rows, local, wide = latent.shape
    count = tiles * blocks
    vmem = pl.BlockSpec(memory_space=pltpu.VMEM)
    hbm = pl.BlockSpec(memory_space=pl.ANY)
    dma = pltpu.SemaphoreType.DMA
    here = lambda v: pltpu.with_memory_space_constraint(v, pltpu.HBM)
    row = lambda v: here(v.reshape(1, local))
    return pl.pallas_call(
        functools.partial(kernel, tiles, blocks),
        out_shape=jax.ShapeDtypeStruct((frames, 2 * rows, local // 4, 2 * wide), BF16),
        in_specs=[hbm] * 9,
        out_specs=vmem,
        scratch_shapes=[
            pltpu.VMEM(w1.shape, BF16),
            pltpu.VMEM(w2.shape, BF16),
            pltpu.VMEM((3, 3 * local, 3 * C), BF16),
            pltpu.VMEM((3, 3 * local, 3 * C), BF16),
            pltpu.VMEM((3, 2, 4, local, wide), BF16),
            pltpu.VMEM((4, 6 * C, wide), BF16),
            pltpu.VMEM((4, 2, local, wide), F32),
            pltpu.VMEM((2, 4, local, wide), BF16),
            pltpu.VMEM((2, 4, local, wide), BF16),
            pltpu.VMEM((4, 4 * C, wide), BF16),
            pltpu.VMEM((4, local, wide), F32),
            pltpu.VMEM((2 * wide, 2 * wide), BF16),
            pltpu.VMEM((6, 1, local), F32),
            pltpu.VMEM((6, local, 128), F32),
            pltpu.VMEM((6, 2, local, 128), F32),
            pltpu.VMEM((2, 1, 128), F32),
            pltpu.VMEM((2, count, 1, 128), F32),
            dma((7,)),
            dma((2,)),
            dma((2, 2, 2)),
            dma((3, 2, 2)),
            dma((3, 4, 2)),
            dma((4, 6)),
            dma((4, 6)),
            dma((2, 4)),
            dma((2, 4)),
            dma((4, 4)),
            dma((4, 4)),
            dma((2, count)),
            dma((2, count)),
        ],
        compiler_params=pltpu.CompilerParams(
            collective_id=0, has_side_effects=True, vmem_limit_bytes=48 * 1024 * 1024
        ),
        name="block",
    )(here(latent), row(n1g), row(n1b), here(w1), row(c1b), row(n2g), row(n2b), here(w2), row(c2b))


def solution(mesh):
    return jax.shard_map(
        functools.partial(shards, mesh.shape["tile"], mesh.shape["tm"]),
        mesh=mesh,
        in_specs=(
            P(("clip", "tm"), "tile", "chan", None),
            P("chan"),
            P("chan"),
            P(None, None, None, None, "chan"),
            P("chan"),
            P("chan"),
            P("chan"),
            P(None, None, None, None, "chan"),
            P("chan"),
        ),
        out_specs=P(("clip", "tm"), "tile", "chan", None),
        check_vma=False,
    )
```
